32 devices in a mesh: energy: 16 (over z, y, x), slab: 2 (over core).
Axes of the slice: x: 2, y: 2, z: 4, core: 2. Of those that a mesh axis runs over, the one named last changes fastest.
Arguments:
- g_less: bfloat16 [1024, 2, 5, 64, 128], P('energy', 'slab'), may hold values from -6 to 6
- g_greater: bfloat16 [1024, 2, 5, 64, 128], P('energy', 'slab'), may hold values from -6 to 6
- coulomb: bfloat16 [2, 64, 192], P('slab'), may hold values from -0.4375 to 0.4375
- pattern: int32 [2, 5], replicated, may hold values from 0 to 7, as said below
Outputs:
- screened: bfloat16 [1024, 2, 5, 64, 128], P('energy', 'slab')
The draws below stay inside these ranges and needn't reach their ends.
Inputs may be any that keep to these rules, and one draw needn't show every extreme that they name: `pattern`: row r holds 5 distinct columns: r, r + 3, r + 6 and two of r + 1, r + 2, r + 4, r + 5, in any order of slots.
All inputs are finite; a program needn't handle non-finite values.
Results may differ from the reference program's by a relative error of at most 0.007.
Values may be sent and summed in bfloat16 or wider, within the bound.
A program may use at most 128 MiB of HBM per device.

```python
import math
import jax
import jax.numpy as jnp
from jax import lax

NE = 1024
BI = 64
SLOTS = 5
ROWS = 2


def draw_pattern(key, part):
    first_key = jax.random.fold_in(key, 11)
    second_key = jax.random.fold_in(key, 23)
    choices_table = jnp.array([1, 2, 4, 5], dtype=jnp.int32)
    scores = jax.random.randint(first_key, (ROWS, 4), 0, 4096) * 8 + jnp.arange(4, dtype=jnp.int32)[None, :]
    ranking = jnp.argsort(scores, axis=1, stable=True)
    chosen = choices_table[ranking[:, :2]]
    fixed_part = jnp.broadcast_to(jnp.array([0, 3, 6], dtype=jnp.int32)[None, :], (ROWS, 3))
    offsets = jnp.concatenate([fixed_part, chosen], 1)
    order_scores = jax.random.randint(second_key, (ROWS, 5), 0, 4096) * 8 + jnp.arange(5, dtype=jnp.int32)[None, :]
    ordering = jnp.argsort(order_scores, axis=1, stable=True)
    offsets = jnp.take_along_axis(offsets, ordering, axis=1)
    return (jnp.arange(ROWS, dtype=jnp.int32)[:, None] + offsets).astype(jnp.int32)


def block_levels(stream_key, dims, cuts, smallest, top_value):
    level, own = 1.0, jax.random.fold_in(stream_key, 6)
    for axis_at, shards_of in cuts:
        heights = jnp.exp(jax.random.uniform(jax.random.fold_in(own, axis_at), (shards_of,), jnp.float32, smallest / len(cuts), top_value / len(cuts)))
        level = level * jnp.repeat(heights, dims[axis_at] // shards_of).reshape([-1 if axis == axis_at else 1 for axis in range(len(dims))])
    return level


def bell_draw(own_key, shape, scale, bound, pieces=(), held_as=jnp.bfloat16):
    values = jax.random.normal(own_key, shape, jnp.float32) * scale
    if len(pieces) > 0:
        values = block_levels(own_key, shape, pieces, -0.22, 0.18) * values
    return jnp.clip(values, min=-bound, max=bound).astype(held_as)


def setup_inputs(seed: int = 0) -> dict:
    key_list = jax.random.split(jax.random.key(seed), 5)
    g_less = bell_draw(key_list[0], (NE, ROWS, SLOTS, BI, 2 * BI), 1.0, 6.0, ((0, 16), (1, 2)))
    g_greater = bell_draw(key_list[1], (NE, ROWS, SLOTS, BI, 2 * BI), 1.0, 6.0, ((0, 16), (1, 2)))
    coulomb = bell_draw(key_list[2], (ROWS, BI, 3 * BI), (3 * BI) ** -0.5, 0.4375, ((0, 2),))
    pattern = draw_pattern(jax.random.fold_in(key_list[4], 71), 0)
    return {"g_less": g_less, "g_greater": g_greater, "coulomb": coulomb, "pattern": pattern}


def make_tables():
    energy_index = jnp.arange(NE, dtype=jnp.int32)
    phases = energy_index[:, None] * energy_index[None, :] % NE
    angles = phases.astype(jnp.float32) * (2.0 * math.pi / NE)
    norm_scale = 1.0 / math.sqrt(NE)
    table_real = (jnp.cos(angles) * norm_scale).astype(jnp.bfloat16)
    table_imag = (-jnp.sin(angles) * norm_scale).astype(jnp.bfloat16)
    return (table_real, table_imag)

def two_products(values, table_real, table_imag):
    flat = values.reshape(NE, -1).astype(jnp.float32)
    direct = jnp.dot(table_real.astype(jnp.float32), flat, preferred_element_type=jnp.float32).reshape(values.shape)
    swapped = jnp.dot(table_imag.astype(jnp.float32), flat, preferred_element_type=jnp.float32).reshape(values.shape)
    return (direct, swapped)

def reference(g_less, g_greater, coulomb, pattern):
    table_real, table_imag = make_tables()
    half_cols = BI

    def polar_row(row_index):
        lesser = lax.dynamic_index_in_dim(g_less, row_index, 1, keepdims=False)
        greater = lax.dynamic_index_in_dim(g_greater, row_index, 1, keepdims=False)
        direct, swapped = two_products(lesser, table_real, table_imag)
        less_real = direct[..., :half_cols] - swapped[..., half_cols:]
        less_imag = direct[..., half_cols:] + swapped[..., :half_cols]
        direct, swapped = two_products(greater, table_real, table_imag)
        great_real = direct[..., :half_cols] - swapped[..., half_cols:]
        great_imag = direct[..., half_cols:] + swapped[..., :half_cols]
        prod_real = less_real * great_real + less_imag * great_imag
        prod_imag = less_imag * great_real - less_real * great_imag
        product = jnp.concatenate([prod_real, prod_imag], -1).astype(jnp.bfloat16)
        direct, swapped = two_products(product, table_real, table_imag)
        back_real = direct[..., :half_cols] + swapped[..., half_cols:]
        back_imag = direct[..., half_cols:] - swapped[..., :half_cols]
        return jnp.concatenate([back_real, back_imag], -1).astype(jnp.bfloat16)
    polar = jnp.moveaxis(lax.map(polar_row, jnp.arange(ROWS, dtype=jnp.int32)), 0, 1)
    padded = jnp.pad(polar, ((0, 0), (1, 1), (0, 0), (0, 0), (0, 0)))
    filler = jnp.full((1, SLOTS), -1, jnp.int32)
    extended = jnp.concatenate([filler, pattern.astype(jnp.int32), filler], 0)

    def screen_row(row_index):
        neighbours = lax.dynamic_slice_in_dim(padded, row_index, 3, 1).astype(jnp.float32)
        columns = lax.dynamic_slice_in_dim(extended, row_index, 3, 0)
        selector = (columns[:, None, :] == columns[1][None, :, None]).astype(jnp.float32)
        picked = jnp.einsum('dst,edtin->edsin', selector, neighbours)
        weights = lax.dynamic_index_in_dim(coulomb, row_index, 0, keepdims=False)
        weights = weights.reshape(BI, 3, BI).astype(jnp.float32)
        return jnp.einsum('adi,edsin->esan', weights, picked).astype(jnp.bfloat16)
    screened = lax.map(screen_row, jnp.arange(ROWS, dtype=jnp.int32))
    return jnp.moveaxis(screened, 0, 1)
```

```python
import functools
import math

import jax
import jax.numpy as jnp
import numpy as np
from jax import lax
from jax.experimental import pallas as pl
from jax.experimental.pallas import tpu as pltpu
from jax.sharding import PartitionSpec as P

MESH = pl.DeviceIdType.MESH
LANES = 128
TILE = 16


def make_tables(count):
    index = np.arange(count)
    angles = (index[:, None] * index[None, :] % count) * (2.0 * math.pi / count)
    scale = 1.0 / math.sqrt(count)
    table_real = (np.cos(angles) * scale).astype(np.float32).astype(jnp.bfloat16)
    table_imag = (-np.sin(angles) * scale).astype(np.float32).astype(jnp.bfloat16)
    return table_real, table_imag


def split_tables(count, radix):
    part = count // radix
    cut = np.stack(make_tables(count))[:, :part, :].reshape(2, part, part, radix)
    return np.ascontiguousarray(cut.transpose(0, 3, 1, 2)), np.ascontiguousarray(cut.transpose(0, 3, 2, 1))


def turn(values, sign):
    return sign * pltpu.roll(values, LANES // 2, 1)


def guarded(there, action):
    if there is None:
        action()
    else:
        pl.when(there)(action)


def exchange_kernel(
    peers, count, radix, less_hbm, great_hbm, coulomb_hbm, pattern_hbm, fwd_hbm, inv_hbm, out_ref,
    stage, send, held, reply, back, own, near, fwd_ref, inv_ref, coulomb_ref, pattern_ref, weights,
    load_sem, side_sem, send_sem, recv_sem, back_send, back_recv, near_send, near_recv,
):
    me = lax.axis_index("energy")
    row = lax.axis_index("slab")
    slots = send.shape[1]
    local = send.shape[4]
    wide = send.shape[5]
    quads = wide // LANES
    orbitals = stage.shape[3]
    sides = min(count - 1, 2)
    has_below, has_above = row > 0, row < count - 1

    if count == 2:
        origins = ((None, 1 - row, 2 - 2 * row),)
        links = ((None, 1 - row, 0),)
    elif count > 2:
        origins = (
            (has_below, lax.rem(row + count - 1, count), 0),
            (has_above, lax.rem(row + 1, count), 2),
        )
        links = ((has_above, row + 1, 0), (has_below, row - 1, 1))
    else:
        origins, links = (), ()

    barrier = pltpu.get_barrier_semaphore()
    half = peers // 2

    def partner(step):
        if peers & (peers - 1):
            return lax.rem(me + step + 1, peers)
        odd = lax.rem(step, 2)
        mask = (1 - odd) * half + lax.div(step + odd, 2)
        peer, bit = 0, 1
        while bit < peers:
            peer = peer + bit * lax.rem(lax.div(me, bit) + lax.div(mask, bit), 2)
            bit *= 2
        return peer

    def greet(step, carry):
        pl.semaphore_signal(
            barrier, inc=1, device_id={"energy": partner(step)}, device_id_type=MESH
        )
        return carry

    def load(which, slot, buf):
        source = (less_hbm, great_hbm)[which]
        return pltpu.make_async_copy(source.at[:, :, slot], stage.at[buf], load_sem.at[buf])

    lax.fori_loop(0, peers - 1, greet, 0)
    greeted = peers - 1
    for there, peer, _ in links:
        def meet(peer=peer):
            pl.semaphore_signal(barrier, inc=1, device_id={"slab": peer}, device_id_type=MESH)

        guarded(there, meet)
        greeted = greeted + (1 if there is None else there.astype(jnp.int32))

    load(0, 0, 0).start()
    fetches = [
        pltpu.make_async_copy(source, target, side_sem.at[k])
        for k, (source, target) in enumerate(
            (
                (fwd_hbm, fwd_ref), (inv_hbm, inv_ref),
                (coulomb_hbm, coulomb_ref), (pattern_hbm, pattern_ref),
            )
        )
    ]

    lane = lax.broadcasted_iota(jnp.int32, (1, LANES), 1)
    sign = jnp.where(lane < LANES // 2, -1.0, 1.0).astype(jnp.float32)
    mine = pl.ds(pl.multiple_of(me * local, local), local)

    def scatter(which, slot):
        load(which, slot, which).wait()
        if which == 0:
            load(1, slot, 1).start()
        else:
            @pl.when(slot + 1 < slots)
            def _():
                load(0, slot + 1, 0).start()

        def cut(group, carry):
            top = pl.multiple_of(group * TILE, TILE)
            for r in range(radix):
                tile = stage[which, :, r, pl.ds(top, TILE), :].astype(jnp.float32)
                tile = jnp.swapaxes(tile, 0, 1).astype(jnp.bfloat16)
                for k in range(TILE):
                    send[which, slot, group * (TILE // quads) + k // quads, r, :,
                         (k % quads) * LANES : (k % quads + 1) * LANES] = tile[k]
            return carry

        lax.fori_loop(0, orbitals // TILE, cut, 0)
        if which == 0:
            @pl.when(slot == 0)
            def _():
                for fetch in fetches:
                    fetch.start()
                pl.semaphore_wait(barrier, greeted)

        def ship(step, carry):
            peer = partner(step)
            pltpu.make_async_remote_copy(
                src_ref=send.at[which, slot, peer],
                dst_ref=held.at[which, slot, :, mine, :],
                send_sem=send_sem.at[which, slot],
                recv_sem=recv_sem.at[which, slot],
                device_id={"energy": peer},
                device_id_type=MESH,
            ).start()
            return carry

        lax.fori_loop(0, peers - 1, ship, 0)
        pltpu.make_async_copy(
            send.at[which, slot, me], held.at[which, slot, :, mine, :], recv_sem.at[which, slot]
        ).start()

    def scatter_slot(slot, carry):
        scatter(0, slot)
        scatter(1, slot)
        return carry

    lax.fori_loop(0, slots, scatter_slot, 0)
    for fetch in fetches:
        fetch.wait()

    span = orbitals * (1 + sides)
    depth = slots * span
    entry = lax.broadcasted_iota(jnp.int32, (3 * orbitals, depth), 0)
    place = lax.broadcasted_iota(jnp.int32, (1, depth), 1)
    block = place // orbitals
    inner = lax.rem(place, orbitals)
    column = jnp.full((1, depth), -1, jnp.int32)
    piece = jnp.full((1, depth), 1, jnp.int32)
    for t in range(slots):
        at = t * (1 + sides)
        column = jnp.where(block == at, pattern_ref[row, t], column)
        for side, (there, k, d) in enumerate(origins):
            there = 1 if there is None else there.astype(jnp.int32)
            seen = there * (pattern_ref[k, t] + 1) - 1
            column = jnp.where(block == at + 1 + side, seen, column)
            piece = jnp.where(block == at + 1 + side, d, piece)
    wanted = lax.rem(inner, peers) * quads + inner // peers + piece * orbitals
    for s in range(slots):
        goal = jnp.where(column == pattern_ref[row, s], wanted, -1)
        select = (entry == goal).astype(jnp.float32).astype(jnp.bfloat16)
        part_of = jnp.dot(coulomb_ref[...], select, preferred_element_type=jnp.float32)
        weights[s * orbitals : (s + 1) * orbitals, :] = part_of.astype(jnp.bfloat16)

    for side, (there, _, _) in enumerate(origins):
        if there is not None:
            @pl.when(jnp.logical_not(there))
            def _(side=side):
                near[side] = jnp.zeros(near.shape[1:], near.dtype)

    def forward(which, slot, col):
        pieces = []
        for r in range(radix):
            block = held[which, slot, r, :, col]
            direct = jnp.dot(fwd_ref[0, r], block, preferred_element_type=jnp.float32)
            crossed = jnp.dot(fwd_ref[1, r], block, preferred_element_type=jnp.float32)
            pieces.append(direct + turn(crossed, sign))
        if radix == 1:
            return pieces
        even, odd = pieces[0] + pieces[2], pieces[1] + pieces[3]
        gap, twist = pieces[0] - pieces[2], turn(pieces[1] - pieces[3], sign)
        return [even + odd, gap - twist, even - odd, gap + twist]

    def compute(slot, carry):
        for which in range(2):
            pltpu.make_async_copy(
                held.at[which, slot], held.at[which, slot], recv_sem.at[which, slot]
            ).wait()
        for quad in range(quads):
            col = slice(quad * LANES, (quad + 1) * LANES)
            lesser = forward(0, slot, col)
            greater = forward(1, slot, col)
            products = []
            for a, b in zip(lesser, greater):
                along = a * b
                across = a * pltpu.roll(b, LANES // 2, 1)
                products.append(
                    jnp.where(
                        lane < LANES // 2,
                        along + pltpu.roll(along, LANES // 2, 1),
                        across - pltpu.roll(across, LANES // 2, 1),
                    )
                )
            if radix == 4:
                z0, z1, z2, z3 = products
                even, odd = z0 + z2, z1 + z3
                gap, twist = z0 - z2, turn(z1 - z3, sign)
                products = [even + odd, gap + twist, even - odd, gap - twist]
            for r in range(radix):
                block = products[r].astype(jnp.bfloat16)
                direct = jnp.dot(inv_ref[0, r], block, preferred_element_type=jnp.float32)
                crossed = jnp.dot(inv_ref[1, r], block, preferred_element_type=jnp.float32)
                reply[slot, r, :, col] = (direct - turn(crossed, sign)).astype(jnp.bfloat16)

        for r in range(radix):
            def ship(step, carry, r=r):
                peer = partner(step)
                rows = pl.ds(pl.multiple_of(peer * local, local), local)
                pltpu.make_async_remote_copy(
                    src_ref=reply.at[slot, r, rows, :],
                    dst_ref=back.at[slot, r, me],
                    send_sem=back_send.at[slot],
                    recv_sem=back_recv.at[slot, r],
                    device_id={"energy": peer},
                    device_id_type=MESH,
                ).start()
                return carry

            lax.fori_loop(0, peers - 1, ship, 0)
            pltpu.make_async_copy(
                reply.at[slot, r, mine, :], back.at[slot, r, me], back_recv.at[slot, r]
            ).start()
        return carry

    lax.fori_loop(0, slots, compute, 0)

    def hand(link, slot, r):
        _, peer, side = links[link]
        return pltpu.make_async_remote_copy(
            src_ref=own.at[slot, r],
            dst_ref=near.at[side, slot, r],
            send_sem=near_send.at[link, slot, r],
            recv_sem=near_recv.at[side, slot, r],
            device_id={"slab": peer},
            device_id_type=MESH,
        )

    def collect(slot, r):
        pltpu.make_async_copy(back.at[slot, r], back.at[slot, r], back_recv.at[slot, r]).wait()
        for quad in range(quads):
            tile = back[slot, r, :, :, quad * LANES : (quad + 1) * LANES]
            tile = jnp.swapaxes(tile.astype(jnp.float32), 0, 1).astype(jnp.bfloat16)
            own[slot, r, :, quad * peers : (quad + 1) * peers, :] = tile
        for link, (there, _, _) in enumerate(links):
            guarded(there, lambda link=link: hand(link, slot, r).start())

    def screen(r):
        for side, (there, _, _) in enumerate(origins):
            def arrived(side=side):
                for slot in range(slots):
                    block = near.at[side, slot, r]
                    pltpu.make_async_copy(block, block, near_recv.at[side, slot, r]).wait()

            guarded(there, arrived)

        def pair(k, carry):
            columns = []
            for e in (2 * k, 2 * k + 1):
                rows = []
                for slot in range(slots):
                    rows.append(own[slot, r, e])
                    for side in range(sides):
                        rows.append(near[side, slot, r, e])
                columns.append(jnp.concatenate(rows, 0))
            both = jnp.dot(
                weights[...], jnp.concatenate(columns, 1), preferred_element_type=jnp.float32
            ).astype(jnp.bfloat16)
            for j in range(2):
                for slot in range(slots):
                    out_ref[(2 * k + j) * radix + r, 0, slot] = both[
                        slot * orbitals : (slot + 1) * orbitals, j * LANES : (j + 1) * LANES
                    ]
            return carry

        lax.fori_loop(0, local // 2, pair, 0)

    def collect_slot(slot, carry):
        for r in range(radix):
            collect(slot, r)
        return carry

    lax.fori_loop(0, slots - 1, collect_slot, 0)
    for r in range(radix):
        collect(slots - 1, r)
        if r > 0:
            screen(r - 1)
    screen(radix - 1)

    def finish(slot, carry):
        rest = pl.ds(0, peers - 1)
        for which in range(2):
            pltpu.make_async_copy(
                send.at[which, slot, rest], send.at[which, slot, rest], send_sem.at[which, slot]
            ).wait()
        pltpu.make_async_copy(
            send.at[0, slot, rest], send.at[0, slot, rest], back_send.at[slot]
        ).wait()
        for link, (there, _, _) in enumerate(links):
            def gone(link=link):
                for r in range(radix):
                    hand(link, slot, r).wait_send()

            guarded(there, gone)
        return carry

    lax.fori_loop(0, slots, finish, 0)


def shards(g_less, g_greater, coulomb, pattern):
    e_local, _, slots, orbitals, cols = g_less.shape
    peers, rows = lax.axis_size("energy"), lax.axis_size("slab")
    count = e_local * peers
    radix = 4 if e_local % 64 == 0 else 1
    part = count // radix
    local = e_local // radix
    wide = orbitals // peers * cols
    sides = min(rows - 1, 2)
    forward, inverse = split_tables(count, radix)
    shape = (local, radix, slots, orbitals, cols)
    hbm = pl.BlockSpec(memory_space=pltpu.HBM)
    bf16 = jnp.bfloat16
    dma = pltpu.SemaphoreType.DMA
    operands = (g_less.reshape(shape), g_greater.reshape(shape), coulomb[0], pattern, forward, inverse)
    pin = lambda array: pltpu.with_memory_space_constraint(array, pltpu.HBM)
    out = pl.pallas_call(
        functools.partial(exchange_kernel, peers, rows, radix),
        out_shape=jax.ShapeDtypeStruct(g_less.shape, bf16),
        in_specs=[hbm] * 6,
        out_specs=pl.BlockSpec(memory_space=pltpu.VMEM),
        scratch_shapes=[
            pltpu.VMEM((2, local, radix, orbitals, cols), bf16),
            pltpu.VMEM((2, slots, peers, radix, local, wide), bf16),
            pltpu.VMEM((2, slots, radix, part, wide), bf16),
            pltpu.VMEM((slots, radix, part, wide), bf16),
            pltpu.VMEM((slots, radix, peers, local, wide), bf16),
            pltpu.VMEM((slots, radix, local, orbitals, cols), bf16),
            pltpu.VMEM((max(sides, 1), slots, radix, local, orbitals, cols), bf16),
            pltpu.VMEM(forward.shape, bf16),
            pltpu.VMEM(inverse.shape, bf16),
            pltpu.VMEM(coulomb.shape[1:], bf16),
            pltpu.SMEM(pattern.shape, jnp.int32),
            pltpu.VMEM((slots * orbitals, slots * orbitals * (1 + sides)), bf16),
            dma((2,)), dma((4,)), dma((2, slots)), dma((2, slots)), dma((slots,)),
            dma((slots, radix)), dma((max(sides, 1), slots, radix)),
            dma((max(sides, 1), slots, radix)),
        ],
        compiler_params=pltpu.CompilerParams(
            collective_id=0, has_side_effects=True, vmem_limit_bytes=47 * 1024 * 1024
        ),
        name="exchange",
    )(*map(pin, operands))
    return out


def solution(mesh):
    placed = (
        P("energy", "slab", None, None, None),
        P("energy", "slab", None, None, None),
        P("slab", None, None),
        P(),
    )
    return jax.shard_map(
        shards,
        mesh=mesh,
        in_specs=placed,
        out_specs=P("energy", "slab", None, None, None),
        check_vma=False,
    )
```

```python
import functools
import math

import jax
import jax.numpy as jnp
import numpy as np
from jax import lax
from jax.experimental import pallas as pl
from jax.experimental.pallas import tpu as pltpu
from jax.sharding import PartitionSpec as P

MESH = pl.DeviceIdType.MESH
LANES = 128
TILE = 16


def make_tables(count):
    index = np.arange(count)
    angles = (index[:, None] * index[None, :] % count) * (2.0 * math.pi / count)
    scale = 1.0 / math.sqrt(count)
    table_real = (np.cos(angles) * scale).astype(np.float32).astype(jnp.bfloat16)
    table_imag = (-np.sin(angles) * scale).astype(np.float32).astype(jnp.bfloat16)
    return table_real, table_imag


def split_tables(count, radix):
    part = count // radix
    cut = np.stack(make_tables(count))[:, :part, :].reshape(2, part, part, radix)
    return np.ascontiguousarray(cut.transpose(0, 3, 1, 2)), np.ascontiguousarray(cut.transpose(0, 3, 2, 1))


def turn(values, sign):
    return sign * pltpu.roll(values, LANES // 2, 1)


def guarded(there, action):
    if there is None:
        action()
    else:
        pl.when(there)(action)


def exchange_kernel(
    peers, count, radix, less_hbm, great_hbm, coulomb_hbm, pattern_hbm, fwd_hbm, inv_hbm, out_ref,
    stage, send, held, reply, back, own, near, fwd_ref, inv_ref, coulomb_ref, pattern_ref, weights,
    load_sem, side_sem, send_sem, recv_sem, back_send, back_recv, near_send, near_recv,
):
    me = lax.axis_index("energy")
    row = lax.axis_index("slab")
    slots = send.shape[1]
    local = send.shape[4]
    wide = send.shape[5]
    quads = wide // LANES
    orbitals = stage.shape[3]
    sides = min(count - 1, 2)
    has_below, has_above = row > 0, row < count - 1

    if count == 2:
        origins = ((None, 1 - row, 2 - 2 * row),)
        links = ((None, 1 - row, 0),)
    elif count > 2:
        origins = (
            (has_below, lax.rem(row + count - 1, count), 0),
            (has_above, lax.rem(row + 1, count), 2),
        )
        links = ((has_above, row + 1, 0), (has_below, row - 1, 1))
    else:
        origins, links = (), ()

    barrier = pltpu.get_barrier_semaphore()
    half = peers // 2

    def partner(step):
        if peers & (peers - 1):
            return lax.rem(me + step + 1, peers)
        odd = lax.rem(step, 2)
        mask = (1 - odd) * half + lax.div(step + odd, 2)
        peer, bit = 0, 1
        while bit < peers:
            peer = peer + bit * lax.rem(lax.div(me, bit) + lax.div(mask, bit), 2)
            bit *= 2
        return peer

    def greet(step, carry):
        pl.semaphore_signal(
            barrier, inc=1, device_id={"energy": partner(step)}, device_id_type=MESH
        )
        return carry

    def load(which, slot, buf):
        source = (less_hbm, great_hbm)[which]
        return pltpu.make_async_copy(source.at[:, :, slot], stage.at[buf], load_sem.at[buf])

    lax.fori_loop(0, peers - 1, greet, 0)
    greeted = peers - 1
    for there, peer, _ in links:
        def meet(peer=peer):
            pl.semaphore_signal(barrier, inc=1, device_id={"slab": peer}, device_id_type=MESH)

        guarded(there, meet)
        greeted = greeted + (1 if there is None else there.astype(jnp.int32))

    load(0, 0, 0).start()
    fetches = [
        pltpu.make_async_copy(source, target, side_sem.at[k])
        for k, (source, target) in enumerate(
            (
                (fwd_hbm, fwd_ref), (inv_hbm, inv_ref),
                (coulomb_hbm, coulomb_ref), (pattern_hbm, pattern_ref),
            )
        )
    ]

    lane = lax.broadcasted_iota(jnp.int32, (1, LANES), 1)
    sign = jnp.where(lane < LANES // 2, -1.0, 1.0).astype(jnp.float32)
    mine = pl.ds(pl.multiple_of(me * local, local), local)

    def scatter(which, slot):
        load(which, slot, which).wait()
        if which == 0:
            load(1, slot, 1).start()
        else:
            @pl.when(slot + 1 < slots)
            def _():
                load(0, slot + 1, 0).start()

        def cut(group, carry):
            top = pl.multiple_of(group * TILE, TILE)
            for r in range(radix):
                tile = stage[which, :, r, pl.ds(top, TILE), :].astype(jnp.float32)
                tile = jnp.swapaxes(tile, 0, 1).astype(jnp.bfloat16)
                for k in range(TILE):
                    send[which, slot, group * (TILE // quads) + k // quads, r, :,
                         (k % quads) * LANES : (k % quads + 1) * LANES] = tile[k]
            return carry

        lax.fori_loop(0, orbitals // TILE, cut, 0)
        if which == 0:
            @pl.when(slot == 0)
            def _():
                for fetch in fetches:
                    fetch.start()
                pl.semaphore_wait(barrier, greeted)

        def ship(step, carry):
            peer = partner(step)
            pltpu.make_async_remote_copy(
                src_ref=send.at[which, slot, peer],
                dst_ref=held.at[which, slot, :, mine, :],
                send_sem=send_sem.at[which],
                recv_sem=recv_sem.at[which, slot],
                device_id={"energy": peer},
                device_id_type=MESH,
            ).start()
            return carry

        lax.fori_loop(0, peers - 1, ship, 0)
        pltpu.make_async_copy(
            send.at[which, slot, me], held.at[which, slot, :, mine, :], recv_sem.at[which, slot]
        ).start()

    def scatter_slot(slot, carry):
        scatter(0, slot)
        scatter(1, slot)
        return carry

    lax.fori_loop(0, slots, scatter_slot, 0)
    for fetch in fetches:
        fetch.wait()

    span = orbitals * (1 + sides)
    depth = slots * span
    entry = lax.broadcasted_iota(jnp.int32, (3 * orbitals, depth), 0)
    place = lax.broadcasted_iota(jnp.int32, (1, depth), 1)
    block = place // orbitals
    inner = lax.rem(place, orbitals)
    column = jnp.full((1, depth), -1, jnp.int32)
    piece = jnp.full((1, depth), 1, jnp.int32)
    for t in range(slots):
        at = t * (1 + sides)
        column = jnp.where(block == at, pattern_ref[row, t], column)
        for side, (there, k, d) in enumerate(origins):
            there = 1 if there is None else there.astype(jnp.int32)
            seen = there * (pattern_ref[k, t] + 1) - 1
            column = jnp.where(block == at + 1 + side, seen, column)
            piece = jnp.where(block == at + 1 + side, d, piece)
    wanted = lax.rem(inner, peers) * quads + inner // peers + piece * orbitals
    for s in range(slots):
        goal = jnp.where(column == pattern_ref[row, s], wanted, -1)
        select = (entry == goal).astype(jnp.float32).astype(jnp.bfloat16)
        part_of = jnp.dot(coulomb_ref[...], select, preferred_element_type=jnp.float32)
        weights[s * orbitals : (s + 1) * orbitals, :] = part_of.astype(jnp.bfloat16)

    for side, (there, _, _) in enumerate(origins):
        if there is not None:
            @pl.when(jnp.logical_not(there))
            def _(side=side):
                near[side] = jnp.zeros(near.shape[1:], near.dtype)

    def forward(which, slot, col):
        pieces = []
        for r in range(radix):
            block = held[which, slot, r, :, col]
            direct = jnp.dot(fwd_ref[0, r], block, preferred_element_type=jnp.float32)
            crossed = jnp.dot(fwd_ref[1, r], block, preferred_element_type=jnp.float32)
            pieces.append(direct + turn(crossed, sign))
        if radix == 1:
            return pieces
        even, odd = pieces[0] + pieces[2], pieces[1] + pieces[3]
        gap, twist = pieces[0] - pieces[2], turn(pieces[1] - pieces[3], sign)
        return [even + odd, gap - twist, even - odd, gap + twist]

    def compute(slot, carry):
        for which in range(2):
            pltpu.make_async_copy(
                held.at[which, slot], held.at[which, slot], recv_sem.at[which, slot]
            ).wait()
        for quad in range(quads):
            col = slice(quad * LANES, (quad + 1) * LANES)
            lesser = forward(0, slot, col)
            greater = forward(1, slot, col)
            products = []
            for a, b in zip(lesser, greater):
                along = a * b
                across = a * pltpu.roll(b, LANES // 2, 1)
                products.append(
                    jnp.where(
                        lane < LANES // 2,
                        along + pltpu.roll(along, LANES // 2, 1),
                        across - pltpu.roll(across, LANES // 2, 1),
                    )
                )
            if radix == 4:
                z0, z1, z2, z3 = products
                even, odd = z0 + z2, z1 + z3
                gap, twist = z0 - z2, turn(z1 - z3, sign)
                products = [even + odd, gap + twist, even - odd, gap - twist]
            for r in range(radix):
                block = products[r].astype(jnp.bfloat16)
                direct = jnp.dot(inv_ref[0, r], block, preferred_element_type=jnp.float32)
                crossed = jnp.dot(inv_ref[1, r], block, preferred_element_type=jnp.float32)
                reply[slot, r, :, col] = (direct - turn(crossed, sign)).astype(jnp.bfloat16)

        for r in range(radix):
            def ship(step, carry, r=r):
                peer = partner(step)
                rows = pl.ds(pl.multiple_of(peer * local, local), local)
                pltpu.make_async_remote_copy(
                    src_ref=reply.at[slot, r, rows, :],
                    dst_ref=back.at[slot, r, me],
                    send_sem=back_send.at[0],
                    recv_sem=back_recv.at[slot, r],
                    device_id={"energy": peer},
                    device_id_type=MESH,
                ).start()
                return carry

            lax.fori_loop(0, peers - 1, ship, 0)
            pltpu.make_async_copy(
                reply.at[slot, r, mine, :], back.at[slot, r, me], back_recv.at[slot, r]
            ).start()
        return carry

    lax.fori_loop(0, slots, compute, 0)

    def hand(link, slot, r):
        _, peer, side = links[link]
        return pltpu.make_async_remote_copy(
            src_ref=own.at[slot, r],
            dst_ref=near.at[side, slot, r],
            send_sem=near_send.at[link],
            recv_sem=near_recv.at[side, r],
            device_id={"slab": peer},
            device_id_type=MESH,
        )

    def collect(slot, r):
        pltpu.make_async_copy(back.at[slot, r], back.at[slot, r], back_recv.at[slot, r]).wait()
        for quad in range(quads):
            tile = back[slot, r, :, :, quad * LANES : (quad + 1) * LANES]
            tile = jnp.swapaxes(tile.astype(jnp.float32), 0, 1).astype(jnp.bfloat16)
            own[slot, r, :, quad * peers : (quad + 1) * peers, :] = tile
        for link, (there, _, _) in enumerate(links):
            guarded(there, lambda link=link: hand(link, slot, r).start())

    def screen(r):
        for side, (there, _, _) in enumerate(origins):
            def arrived(side=side):
                block = near.at[side, :, r]
                pltpu.make_async_copy(block, block, near_recv.at[side, r]).wait()

            guarded(there, arrived)

        for first in range(0, local, 2):
            columns = []
            for e in (first, first + 1):
                rows = []
                for slot in range(slots):
                    rows.append(own[slot, r, e])
                    for side in range(sides):
                        rows.append(near[side, slot, r, e])
                columns.append(jnp.concatenate(rows, 0))
            both = jnp.dot(
                weights[...], jnp.concatenate(columns, 1), preferred_element_type=jnp.float32
            ).astype(jnp.bfloat16)
            for j in range(2):
                for slot in range(slots):
                    out_ref[(first + j) * radix + r, 0, slot] = both[
                        slot * orbitals : (slot + 1) * orbitals, j * LANES : (j + 1) * LANES
                    ]

    def collect_slot(slot, carry):
        for r in range(radix):
            collect(slot, r)
        return carry

    lax.fori_loop(0, slots - 1, collect_slot, 0)
    rest = pl.ds(0, peers - 1)
    for which in range(2):
        pltpu.make_async_copy(
            send.at[which, :, rest], send.at[which, :, rest], send_sem.at[which]
        ).wait()
    for r in range(radix):
        collect(slots - 1, r)
        if r > 0:
            screen(r - 1)
    screen(radix - 1)
    pltpu.make_async_copy(send.at[0, :, rest], send.at[0, :, rest], back_send.at[0]).wait()
    for link, (there, _, _) in enumerate(links):
        guarded(there, pltpu.make_async_copy(own, own, near_send.at[link]).wait)


def shards(g_less, g_greater, coulomb, pattern):
    e_local, _, slots, orbitals, cols = g_less.shape
    peers, rows = lax.axis_size("energy"), lax.axis_size("slab")
    count = e_local * peers
    radix = 4 if e_local % 64 == 0 else 1
    part = count // radix
    local = e_local // radix
    wide = orbitals // peers * cols
    sides = min(rows - 1, 2)
    forward, inverse = split_tables(count, radix)
    shape = (local, radix, slots, orbitals, cols)
    hbm = pl.BlockSpec(memory_space=pltpu.HBM)
    bf16 = jnp.bfloat16
    dma = pltpu.SemaphoreType.DMA
    operands = (g_less.reshape(shape), g_greater.reshape(shape), coulomb[0], pattern, forward, inverse)
    pin = lambda array: pltpu.with_memory_space_constraint(array, pltpu.HBM)
    out = pl.pallas_call(
        functools.partial(exchange_kernel, peers, rows, radix),
        out_shape=jax.ShapeDtypeStruct(g_less.shape, bf16),
        in_specs=[hbm] * 6,
        out_specs=pl.BlockSpec(memory_space=pltpu.VMEM),
        scratch_shapes=[
            pltpu.VMEM((2, local, radix, orbitals, cols), bf16),
            pltpu.VMEM((2, slots, peers, radix, local, wide), bf16),
            pltpu.VMEM((2, slots, radix, part, wide), bf16),
            pltpu.VMEM((slots, radix, part, wide), bf16),
            pltpu.VMEM((slots, radix, peers, local, wide), bf16),
            pltpu.VMEM((slots, radix, local, orbitals, cols), bf16),
            pltpu.VMEM((max(sides, 1), slots, radix, local, orbitals, cols), bf16),
            pltpu.VMEM(forward.shape, bf16),
            pltpu.VMEM(inverse.shape, bf16),
            pltpu.VMEM(coulomb.shape[1:], bf16),
            pltpu.SMEM(pattern.shape, jnp.int32),
            pltpu.VMEM((slots * orbitals, slots * orbitals * (1 + sides)), bf16),
            dma((2,)), dma((4,)), dma((2,)), dma((2, slots)), dma((1,)), dma((slots, radix)),
            dma((max(sides, 1),)), dma((max(sides, 1), radix)),
        ],
        compiler_params=pltpu.CompilerParams(
            collective_id=0, has_side_effects=True, vmem_limit_bytes=47 * 1024 * 1024
        ),
        name="exchange",
    )(*map(pin, operands))
    return out


def solution(mesh):
    placed = (
        P("energy", "slab", None, None, None),
        P("energy", "slab", None, None, None),
        P("slab", None, None),
        P(),
    )
    return jax.shard_map(
        shards,
        mesh=mesh,
        in_specs=placed,
        out_specs=P("energy", "slab", None, None, None),
        check_vma=False,
    )
```

```python
import functools
import math

import jax
import jax.numpy as jnp
import numpy as np
from jax import lax
from jax.experimental import pallas as pl
from jax.experimental.pallas import tpu as pltpu
from jax.sharding import PartitionSpec as P

MESH = pl.DeviceIdType.MESH
LANES = 128
TILE = 16


def make_tables(count):
    index = np.arange(count)
    angles = (index[:, None] * index[None, :] % count) * (2.0 * math.pi / count)
    scale = 1.0 / math.sqrt(count)
    table_real = (np.cos(angles) * scale).astype(np.float32).astype(jnp.bfloat16)
    table_imag = (-np.sin(angles) * scale).astype(np.float32).astype(jnp.bfloat16)
    return table_real, table_imag


def split_tables(count, radix):
    part = count // radix
    cut = np.stack(make_tables(count))[:, :part, :].reshape(2, part, part, radix)
    return np.ascontiguousarray(cut.transpose(0, 3, 1, 2)), np.ascontiguousarray(cut.transpose(0, 3, 2, 1))


def turn(values, sign):
    return sign * pltpu.roll(values, LANES // 2, 1)


def guarded(there, action):
    if there is None:
        action()
    else:
        pl.when(there)(action)


def exchange_kernel(
    peers, count, radix, less_hbm, great_hbm, coulomb_hbm, pattern_hbm, fwd_hbm, inv_hbm,
    done, own_last, near_last, weights,
    stage, send, held, reply, back, own, near, fwd_ref, inv_ref, coulomb_ref, pattern_ref,
    load_sem, side_sem, send_sem, recv_sem, back_send, back_recv, near_send, near_recv,
):
    me = lax.axis_index("energy")
    row = lax.axis_index("slab")
    slots = send.shape[1]
    local = send.shape[4]
    wide = send.shape[5]
    quads = wide // LANES
    orbitals = stage.shape[3]
    sides = min(count - 1, 2)
    has_below, has_above = row > 0, row < count - 1

    if count == 2:
        origins = ((None, 1 - row, 2 - 2 * row),)
        links = ((None, 1 - row, 0),)
    elif count > 2:
        origins = (
            (has_below, lax.rem(row + count - 1, count), 0),
            (has_above, lax.rem(row + 1, count), 2),
        )
        links = ((has_above, row + 1, 0), (has_below, row - 1, 1))
    else:
        origins, links = (), ()

    barrier = pltpu.get_barrier_semaphore()
    half = peers // 2

    def partner(step):
        if peers & (peers - 1):
            return lax.rem(me + step + 1, peers)
        odd = lax.rem(step, 2)
        mask = (1 - odd) * half + lax.div(step + odd, 2)
        peer, bit = 0, 1
        while bit < peers:
            peer = peer + bit * lax.rem(lax.div(me, bit) + lax.div(mask, bit), 2)
            bit *= 2
        return peer

    def greet(step, carry):
        pl.semaphore_signal(
            barrier, inc=1, device_id={"energy": partner(step)}, device_id_type=MESH
        )
        return carry

    def load(which, slot, buf):
        source = (less_hbm, great_hbm)[which]
        return pltpu.make_async_copy(source.at[:, :, slot], stage.at[buf], load_sem.at[buf])

    lax.fori_loop(0, peers - 1, greet, 0)
    greeted = peers - 1
    for there, peer, _ in links:
        def meet(peer=peer):
            pl.semaphore_signal(barrier, inc=1, device_id={"slab": peer}, device_id_type=MESH)

        guarded(there, meet)
        greeted = greeted + (1 if there is None else there.astype(jnp.int32))

    load(0, 0, 0).start()
    fetches = [
        pltpu.make_async_copy(source, target, side_sem.at[k])
        for k, (source, target) in enumerate(
            (
                (fwd_hbm, fwd_ref), (inv_hbm, inv_ref),
                (coulomb_hbm, coulomb_ref), (pattern_hbm, pattern_ref),
            )
        )
    ]

    lane = lax.broadcasted_iota(jnp.int32, (1, LANES), 1)
    sign = jnp.where(lane < LANES // 2, -1.0, 1.0).astype(jnp.float32)
    mine = pl.ds(pl.multiple_of(me * local, local), local)

    def scatter(which, slot):
        load(which, slot, which).wait()
        if which == 0:
            load(1, slot, 1).start()
        else:
            @pl.when(slot + 1 < slots)
            def _():
                load(0, slot + 1, 0).start()

        def cut(group, carry):
            top = pl.multiple_of(group * TILE, TILE)
            for r in range(radix):
                tile = stage[which, :, r, pl.ds(top, TILE), :].astype(jnp.float32)
                tile = jnp.swapaxes(tile, 0, 1).astype(jnp.bfloat16)
                for k in range(TILE):
                    send[which, slot, group * (TILE // quads) + k // quads, r, :,
                         (k % quads) * LANES : (k % quads + 1) * LANES] = tile[k]
            return carry

        lax.fori_loop(0, orbitals // TILE, cut, 0)
        if which == 0:
            @pl.when(slot == 0)
            def _():
                for fetch in fetches:
                    fetch.start()
                pl.semaphore_wait(barrier, greeted)

        def ship(step, carry):
            peer = partner(step)
            pltpu.make_async_remote_copy(
                src_ref=send.at[which, slot, peer],
                dst_ref=held.at[which, slot, :, mine, :],
                send_sem=send_sem.at[which],
                recv_sem=recv_sem.at[which, slot],
                device_id={"energy": peer},
                device_id_type=MESH,
            ).start()
            return carry

        lax.fori_loop(0, peers - 1, ship, 0)
        pltpu.make_async_copy(
            send.at[which, slot, me], held.at[which, slot, :, mine, :], recv_sem.at[which, slot]
        ).start()

    def scatter_slot(slot, carry):
        scatter(0, slot)
        scatter(1, slot)
        return carry

    lax.fori_loop(0, slots, scatter_slot, 0)
    for fetch in fetches:
        fetch.wait()

    span = orbitals * (1 + sides)
    depth = slots * span
    entry = lax.broadcasted_iota(jnp.int32, (3 * orbitals, depth), 0)
    place = lax.broadcasted_iota(jnp.int32, (1, depth), 1)
    block = place // orbitals
    inner = lax.rem(place, orbitals)
    column = jnp.full((1, depth), -1, jnp.int32)
    piece = jnp.full((1, depth), 1, jnp.int32)
    for t in range(slots):
        at = t * (1 + sides)
        column = jnp.where(block == at, pattern_ref[row, t], column)
        for side, (there, k, d) in enumerate(origins):
            there = 1 if there is None else there.astype(jnp.int32)
            seen = there * (pattern_ref[k, t] + 1) - 1
            column = jnp.where(block == at + 1 + side, seen, column)
            piece = jnp.where(block == at + 1 + side, d, piece)
    wanted = lax.rem(inner, peers) * quads + inner // peers + piece * orbitals
    for s in range(slots):
        goal = jnp.where(column == pattern_ref[row, s], wanted, -1)
        select = (entry == goal).astype(jnp.float32).astype(jnp.bfloat16)
        part_of = jnp.dot(coulomb_ref[...], select, preferred_element_type=jnp.float32)
        weights[s * orbitals : (s + 1) * orbitals, :] = part_of.astype(jnp.bfloat16)

    for side, (there, _, _) in enumerate(origins):
        if there is not None:
            @pl.when(jnp.logical_not(there))
            def _(side=side):
                near[side] = jnp.zeros(near.shape[1:], near.dtype)
                near_last[side] = jnp.zeros(near_last.shape[1:], near_last.dtype)

    def forward(which, slot, col):
        pieces = []
        for r in range(radix):
            block = held[which, slot, r, :, col]
            direct = jnp.dot(fwd_ref[0, r], block, preferred_element_type=jnp.float32)
            crossed = jnp.dot(fwd_ref[1, r], block, preferred_element_type=jnp.float32)
            pieces.append(direct + turn(crossed, sign))
        if radix == 1:
            return pieces
        even, odd = pieces[0] + pieces[2], pieces[1] + pieces[3]
        gap, twist = pieces[0] - pieces[2], turn(pieces[1] - pieces[3], sign)
        return [even + odd, gap - twist, even - odd, gap + twist]

    def compute(slot, carry):
        for which in range(2):
            pltpu.make_async_copy(
                held.at[which, slot], held.at[which, slot], recv_sem.at[which, slot]
            ).wait()
        for quad in range(quads):
            col = slice(quad * LANES, (quad + 1) * LANES)
            lesser = forward(0, slot, col)
            greater = forward(1, slot, col)
            products = []
            for a, b in zip(lesser, greater):
                along = a * b
                across = a * pltpu.roll(b, LANES // 2, 1)
                products.append(
                    jnp.where(
                        lane < LANES // 2,
                        along + pltpu.roll(along, LANES // 2, 1),
                        across - pltpu.roll(across, LANES // 2, 1),
                    )
                )
            if radix == 4:
                z0, z1, z2, z3 = products
                even, odd = z0 + z2, z1 + z3
                gap, twist = z0 - z2, turn(z1 - z3, sign)
                products = [even + odd, gap + twist, even - odd, gap - twist]
            for r in range(radix):
                block = products[r].astype(jnp.bfloat16)
                direct = jnp.dot(inv_ref[0, r], block, preferred_element_type=jnp.float32)
                crossed = jnp.dot(inv_ref[1, r], block, preferred_element_type=jnp.float32)
                reply[slot, r, :, col] = (direct - turn(crossed, sign)).astype(jnp.bfloat16)

        for r in range(radix):
            def ship(step, carry, r=r):
                peer = partner(step)
                rows = pl.ds(pl.multiple_of(peer * local, local), local)
                pltpu.make_async_remote_copy(
                    src_ref=reply.at[slot, r, rows, :],
                    dst_ref=back.at[slot, r, me],
                    send_sem=back_send.at[0],
                    recv_sem=back_recv.at[slot, r],
                    device_id={"energy": peer},
                    device_id_type=MESH,
                ).start()
                return carry

            lax.fori_loop(0, peers - 1, ship, 0)
            pltpu.make_async_copy(
                reply.at[slot, r, mine, :], back.at[slot, r, me], back_recv.at[slot, r]
            ).start()
        return carry

    lax.fori_loop(0, slots, compute, 0)

    last = radix - 1

    def hand(link, slot, r):
        _, peer, side = links[link]
        return pltpu.make_async_remote_copy(
            src_ref=own_last.at[slot] if r == last else own.at[slot, r],
            dst_ref=near_last.at[side, slot] if r == last else near.at[side, slot, r],
            send_sem=near_send.at[link, r],
            recv_sem=near_recv.at[side, r],
            device_id={"slab": peer},
            device_id_type=MESH,
        )

    def collect(slot, r):
        pltpu.make_async_copy(back.at[slot, r], back.at[slot, r], back_recv.at[slot, r]).wait()
        target = own_last.at[slot] if r == last else own.at[slot, r]
        for quad in range(quads):
            tile = back[slot, r, :, :, quad * LANES : (quad + 1) * LANES]
            tile = jnp.swapaxes(tile.astype(jnp.float32), 0, 1).astype(jnp.bfloat16)
            target[:, quad * peers : (quad + 1) * peers, :] = tile
        for link, (there, _, _) in enumerate(links):
            guarded(there, lambda link=link: hand(link, slot, r).start())

    def arrived(r):
        for side, (there, _, _) in enumerate(origins):
            block = near_last.at[side] if r == last else near.at[side, :, r]
            guarded(there, pltpu.make_async_copy(block, block, near_recv.at[side, r]).wait)

    def handed(r):
        for link, (there, _, _) in enumerate(links):
            guarded(there, pltpu.make_async_copy(own_last, own_last, near_send.at[link, r]).wait)

    def screen(r):
        arrived(r)
        handed(r)
        for first in range(0, local, 2):
            pairs = []
            for e in (first, first + 1):
                rows = []
                for slot in range(slots):
                    rows.append(own[slot, r, e])
                    rows.extend(near[side, slot, r, e] for side in range(sides))
                pairs.append(jnp.concatenate(rows, 0))
            for j, block in enumerate(products(weights, pairs)):
                for slot in range(slots):
                    done[r, first + j, slot] = block[slot * orbitals : (slot + 1) * orbitals]

    def collect_slot(slot, carry):
        for r in range(radix):
            collect(slot, r)
        return carry

    lax.fori_loop(0, slots - 1, collect_slot, 0)
    rest = pl.ds(0, peers - 1)
    for which in range(2):
        pltpu.make_async_copy(
            send.at[which, :, rest], send.at[which, :, rest], send_sem.at[which]
        ).wait()
    for r in range(radix):
        collect(slots - 1, r)
        if r > 0:
            screen(r - 1)
    pltpu.make_async_copy(send.at[0, :, rest], send.at[0, :, rest], back_send.at[0]).wait()
    arrived(last)
    handed(last)


def products(weights, pairs):
    both = jnp.dot(weights[...], jnp.concatenate(pairs, 1), preferred_element_type=jnp.float32)
    both = both.astype(jnp.bfloat16)
    return [both[:, j * LANES : (j + 1) * LANES] for j in range(len(pairs))]


def finish_kernel(done, own_ref, near_ref, weights, out_hbm, tail, copy_sem, tail_sem):
    slots, local, orbitals, _ = own_ref.shape
    sides = near_ref.shape[0] if weights.shape[1] > slots * orbitals else 0
    last = out_hbm.shape[1] - 1
    share = local // 2
    copies = [
        pltpu.make_async_copy(
            done.at[r, pl.ds(half * share, share)],
            out_hbm.at[pl.ds(half * share, share), r],
            copy_sem.at[r, half],
        )
        for r in range(last)
        for half in range(2)
    ]
    for copy in copies:
        copy.start()
    for half in range(2):
        for first in range(half * share, (half + 1) * share, 2):
            pairs = []
            for e in (first, first + 1):
                rows = []
                for slot in range(slots):
                    rows.append(own_ref[slot, e])
                    rows.extend(near_ref[side, slot, e] for side in range(sides))
                pairs.append(jnp.concatenate(rows, 0))
            for j, block in enumerate(products(weights, pairs)):
                for slot in range(slots):
                    tail[first + j, slot] = block[slot * orbitals : (slot + 1) * orbitals]
        some = pl.ds(half * share, share)
        copies.append(
            pltpu.make_async_copy(tail.at[some], out_hbm.at[some, last], tail_sem.at[half])
        )
        copies[-1].start()
    for copy in copies:
        copy.wait()


def shards(g_less, g_greater, coulomb, pattern):
    e_local, _, slots, orbitals, cols = g_less.shape
    peers, rows = lax.axis_size("energy"), lax.axis_size("slab")
    count = e_local * peers
    radix = 4 if e_local % 64 == 0 else 1
    part = count // radix
    local = e_local // radix
    wide = orbitals // peers * cols
    sides = min(rows - 1, 2)
    forward, inverse = split_tables(count, radix)
    shape = (local, radix, slots, orbitals, cols)
    hbm = pl.BlockSpec(memory_space=pltpu.HBM)
    bf16 = jnp.bfloat16
    dma = pltpu.SemaphoreType.DMA
    operands = (g_less.reshape(shape), g_greater.reshape(shape), coulomb[0], pattern, forward, inverse)
    pin = lambda array: pltpu.with_memory_space_constraint(array, pltpu.HBM)
    kept = max(radix - 1, 1)
    vmem = pl.BlockSpec(memory_space=pltpu.VMEM)
    done, own, near, weights = pl.pallas_call(
        functools.partial(exchange_kernel, peers, rows, radix),
        out_shape=[
            jax.ShapeDtypeStruct((kept, local, slots, orbitals, cols), bf16),
            jax.ShapeDtypeStruct((slots, local, orbitals, cols), bf16),
            jax.ShapeDtypeStruct((max(sides, 1), slots, local, orbitals, cols), bf16),
            jax.ShapeDtypeStruct((slots * orbitals, slots * orbitals * (1 + sides)), bf16),
        ],
        in_specs=[hbm] * 6,
        out_specs=[vmem] * 4,
        scratch_shapes=[
            pltpu.VMEM((2, local, radix, orbitals, cols), bf16),
            pltpu.VMEM((2, slots, peers, radix, local, wide), bf16),
            pltpu.VMEM((2, slots, radix, part, wide), bf16),
            pltpu.VMEM((slots, radix, part, wide), bf16),
            pltpu.VMEM((slots, radix, peers, local, wide), bf16),
            pltpu.VMEM((slots, kept, local, orbitals, cols), bf16),
            pltpu.VMEM((max(sides, 1), slots, kept, local, orbitals, cols), bf16),
            pltpu.VMEM(forward.shape, bf16),
            pltpu.VMEM(inverse.shape, bf16),
            pltpu.VMEM(coulomb.shape[1:], bf16),
            pltpu.SMEM(pattern.shape, jnp.int32),
            dma((2,)), dma((4,)), dma((2,)), dma((2, slots)), dma((1,)), dma((slots, radix)),
            dma((max(sides, 1), radix)), dma((max(sides, 1), radix)),
        ],
        compiler_params=pltpu.CompilerParams(
            collective_id=0, has_side_effects=True, vmem_limit_bytes=44 * 1024 * 1024
        ),
        name="exchange",
    )(*map(pin, operands))
    out = pl.pallas_call(
        finish_kernel,
        out_shape=jax.ShapeDtypeStruct(shape, bf16),
        in_specs=[pl.BlockSpec(memory_space=pl.ANY), vmem, vmem, vmem],
        out_specs=pl.BlockSpec(memory_space=pltpu.HBM),
        scratch_shapes=[
            pltpu.VMEM((local, slots, orbitals, cols), bf16), dma((kept, 2)), dma((2,)),
        ],
        compiler_params=pltpu.CompilerParams(vmem_limit_bytes=16 * 1024 * 1024),
        name="finish",
    )(done, own, near, weights)
    return out.reshape(g_less.shape)


def solution(mesh):
    placed = (
        P("energy", "slab", None, None, None),
        P("energy", "slab", None, None, None),
        P("slab", None, None),
        P(),
    )
    return jax.shard_map(
        shards,
        mesh=mesh,
        in_specs=placed,
        out_specs=P("energy", "slab", None, None, None),
        check_vma=False,
    )
```

```python
import functools
import math

import jax
import jax.numpy as jnp
import numpy as np
from jax import lax
from jax.experimental import pallas as pl
from jax.experimental.pallas import tpu as pltpu
from jax.sharding import PartitionSpec as P

MESH = pl.DeviceIdType.MESH
LANES = 128
TILE = 16


def make_tables(count):
    index = np.arange(count)
    angles = (index[:, None] * index[None, :] % count) * (2.0 * math.pi / count)
    scale = 1.0 / math.sqrt(count)
    table_real = (np.cos(angles) * scale).astype(np.float32).astype(jnp.bfloat16)
    table_imag = (-np.sin(angles) * scale).astype(np.float32).astype(jnp.bfloat16)
    return table_real, table_imag


def split_tables(count, radix):
    part = count // radix
    cut = np.stack(make_tables(count))[:, :part, :].reshape(2, part, part, radix)
    return np.ascontiguousarray(cut.transpose(0, 3, 1, 2)), np.ascontiguousarray(cut.transpose(0, 3, 2, 1))


def turn(values, sign):
    return sign * pltpu.roll(values, LANES // 2, 1)


def guarded(there, action):
    if there is None:
        action()
    else:
        pl.when(there)(action)


def exchange_kernel(
    peers, count, radix, less_hbm, great_hbm, coulomb_hbm, pattern_hbm, fwd_hbm, inv_hbm,
    done, own_last, near_last, weights,
    stage, send, held, reply, back, own, near, fwd_ref, inv_ref, coulomb_ref, pattern_ref,
    load_sem, side_sem, send_sem, recv_sem, back_send, back_recv, near_send, near_recv,
):
    me = lax.axis_index("energy")
    row = lax.axis_index("slab")
    slots = send.shape[1]
    local = send.shape[4]
    wide = send.shape[5]
    quads = wide // LANES
    orbitals = stage.shape[3]
    sides = min(count - 1, 2)
    has_below, has_above = row > 0, row < count - 1

    if count == 2:
        origins = ((None, 1 - row, 2 - 2 * row),)
        links = ((None, 1 - row, 0),)
    elif count > 2:
        origins = (
            (has_below, lax.rem(row + count - 1, count), 0),
            (has_above, lax.rem(row + 1, count), 2),
        )
        links = ((has_above, row + 1, 0), (has_below, row - 1, 1))
    else:
        origins, links = (), ()

    barrier = pltpu.get_barrier_semaphore()
    half = peers // 2

    def partner(step):
        if peers & (peers - 1):
            return lax.rem(me + step + 1, peers)
        odd = lax.rem(step, 2)
        mask = (1 - odd) * half + lax.div(step + odd, 2)
        peer, bit = 0, 1
        while bit < peers:
            peer = peer + bit * lax.rem(lax.div(me, bit) + lax.div(mask, bit), 2)
            bit *= 2
        return peer

    def greet(step, carry):
        pl.semaphore_signal(
            barrier, inc=1, device_id={"energy": partner(step)}, device_id_type=MESH
        )
        return carry

    def load(which, slot, buf):
        source = (less_hbm, great_hbm)[which]
        return pltpu.make_async_copy(source.at[:, :, slot], stage.at[buf], load_sem.at[buf])

    lax.fori_loop(0, peers - 1, greet, 0)
    greeted = peers - 1
    for there, peer, _ in links:
        def meet(peer=peer):
            pl.semaphore_signal(barrier, inc=1, device_id={"slab": peer}, device_id_type=MESH)

        guarded(there, meet)
        greeted = greeted + (1 if there is None else there.astype(jnp.int32))

    load(0, 0, 0).start()
    fetches = [
        pltpu.make_async_copy(source, target, side_sem.at[k])
        for k, (source, target) in enumerate(
            (
                (fwd_hbm, fwd_ref), (inv_hbm, inv_ref),
                (coulomb_hbm, coulomb_ref), (pattern_hbm, pattern_ref),
            )
        )
    ]

    lane = lax.broadcasted_iota(jnp.int32, (1, LANES), 1)
    sign = jnp.where(lane < LANES // 2, -1.0, 1.0).astype(jnp.float32)
    mine = pl.ds(pl.multiple_of(me * local, local), local)

    def scatter(which, slot):
        load(which, slot, which).wait()
        if which == 0:
            load(1, slot, 1).start()
        else:
            @pl.when(slot + 1 < slots)
            def _():
                load(0, slot + 1, 0).start()

        def cut(group, carry):
            top = pl.multiple_of(group * TILE, TILE)
            for r in range(radix):
                tile = stage[which, :, r, pl.ds(top, TILE), :].astype(jnp.float32)
                tile = jnp.swapaxes(tile, 0, 1).astype(jnp.bfloat16)
                for k in range(TILE):
                    send[which, slot, group * (TILE // quads) + k // quads, r, :,
                         (k % quads) * LANES : (k % quads + 1) * LANES] = tile[k]
            return carry

        lax.fori_loop(0, orbitals // TILE, cut, 0)
        if which == 0:
            @pl.when(slot == 0)
            def _():
                for fetch in fetches:
                    fetch.start()
                pl.semaphore_wait(barrier, greeted)

        def ship(step, carry):
            peer = partner(step)
            pltpu.make_async_remote_copy(
                src_ref=send.at[which, slot, peer],
                dst_ref=held.at[which, slot, :, mine, :],
                send_sem=send_sem.at[which],
                recv_sem=recv_sem.at[which, slot],
                device_id={"energy": peer},
                device_id_type=MESH,
            ).start()
            return carry

        lax.fori_loop(0, peers - 1, ship, 0)
        pltpu.make_async_copy(
            send.at[which, slot, me], held.at[which, slot, :, mine, :], recv_sem.at[which, slot]
        ).start()

    def scatter_slot(slot, carry):
        scatter(0, slot)
        scatter(1, slot)
        return carry

    lax.fori_loop(0, slots, scatter_slot, 0)
    for fetch in fetches:
        fetch.wait()

    span = orbitals * (1 + sides)
    depth = slots * span
    entry = lax.broadcasted_iota(jnp.int32, (3 * orbitals, depth), 0)
    place = lax.broadcasted_iota(jnp.int32, (1, depth), 1)
    block = place // orbitals
    inner = lax.rem(place, orbitals)
    column = jnp.full((1, depth), -1, jnp.int32)
    piece = jnp.full((1, depth), 1, jnp.int32)
    for t in range(slots):
        at = t * (1 + sides)
        column = jnp.where(block == at, pattern_ref[row, t], column)
        for side, (there, k, d) in enumerate(origins):
            there = 1 if there is None else there.astype(jnp.int32)
            seen = there * (pattern_ref[k, t] + 1) - 1
            column = jnp.where(block == at + 1 + side, seen, column)
            piece = jnp.where(block == at + 1 + side, d, piece)
    wanted = lax.rem(inner, peers) * quads + inner // peers + piece * orbitals
    for s in range(slots):
        goal = jnp.where(column == pattern_ref[row, s], wanted, -1)
        select = (entry == goal).astype(jnp.float32).astype(jnp.bfloat16)
        part_of = jnp.dot(coulomb_ref[...], select, preferred_element_type=jnp.float32)
        weights[s * orbitals : (s + 1) * orbitals, :] = part_of.astype(jnp.bfloat16)

    for side, (there, _, _) in enumerate(origins):
        if there is not None:
            @pl.when(jnp.logical_not(there))
            def _(side=side):
                near[side] = jnp.zeros(near.shape[1:], near.dtype)
                near_last[side] = jnp.zeros(near_last.shape[1:], near_last.dtype)

    def forward(which, slot, col):
        pieces = []
        for r in range(radix):
            block = held[which, slot, r, :, col]
            direct = jnp.dot(fwd_ref[0, r], block, preferred_element_type=jnp.float32)
            crossed = jnp.dot(fwd_ref[1, r], block, preferred_element_type=jnp.float32)
            pieces.append(direct + turn(crossed, sign))
        if radix == 1:
            return pieces
        even, odd = pieces[0] + pieces[2], pieces[1] + pieces[3]
        gap, twist = pieces[0] - pieces[2], turn(pieces[1] - pieces[3], sign)
        return [even + odd, gap - twist, even - odd, gap + twist]

    def compute(slot, carry):
        for which in range(2):
            pltpu.make_async_copy(
                held.at[which, slot], held.at[which, slot], recv_sem.at[which, slot]
            ).wait()
        for quad in range(quads):
            col = slice(quad * LANES, (quad + 1) * LANES)
            lesser = forward(0, slot, col)
            greater = forward(1, slot, col)
            products = []
            for a, b in zip(lesser, greater):
                along = a * b
                across = a * pltpu.roll(b, LANES // 2, 1)
                products.append(
                    jnp.where(
                        lane < LANES // 2,
                        along + pltpu.roll(along, LANES // 2, 1),
                        across - pltpu.roll(across, LANES // 2, 1),
                    )
                )
            if radix == 4:
                z0, z1, z2, z3 = products
                even, odd = z0 + z2, z1 + z3
                gap, twist = z0 - z2, turn(z1 - z3, sign)
                products = [even + odd, gap + twist, even - odd, gap - twist]
            for r in range(radix):
                block = products[r].astype(jnp.bfloat16)
                direct = jnp.dot(inv_ref[0, r], block, preferred_element_type=jnp.float32)
                crossed = jnp.dot(inv_ref[1, r], block, preferred_element_type=jnp.float32)
                reply[slot, r, :, col] = (direct - turn(crossed, sign)).astype(jnp.bfloat16)

        ending = slot == slots - 1

        def answer(peer, r):
            rows = pl.ds(pl.multiple_of(peer * local, local), local)
            pltpu.make_async_remote_copy(
                src_ref=reply.at[slot, r, rows, :],
                dst_ref=back.at[slot, r, me],
                send_sem=back_send.at[0],
                recv_sem=back_recv.at[slot, r],
                device_id={"energy": peer},
                device_id_type=MESH,
            ).start()

        @pl.when(jnp.logical_and(ending, me > 0))
        def _():
            for r in range(radix):
                answer(0, r)

        for r in range(radix):
            def ship(step, carry, r=r):
                peer = partner(step)

                @pl.when(jnp.logical_or(jnp.logical_not(ending), peer > 0))
                def _():
                    answer(peer, r)
                return carry

            lax.fori_loop(0, peers - 1, ship, 0)
            pltpu.make_async_copy(
                reply.at[slot, r, mine, :], back.at[slot, r, me], back_recv.at[slot, r]
            ).start()
        return carry

    lax.fori_loop(0, slots, compute, 0)

    last = radix - 1

    def hand(link, slot, r):
        _, peer, side = links[link]
        return pltpu.make_async_remote_copy(
            src_ref=own_last.at[slot] if r == last else own.at[slot, r],
            dst_ref=near_last.at[side, slot] if r == last else near.at[side, slot, r],
            send_sem=near_send.at[link, r],
            recv_sem=near_recv.at[side, r],
            device_id={"slab": peer},
            device_id_type=MESH,
        )

    def collect(slot, r):
        pltpu.make_async_copy(back.at[slot, r], back.at[slot, r], back_recv.at[slot, r]).wait()
        target = own_last.at[slot] if r == last else own.at[slot, r]
        for quad in range(quads):
            tile = back[slot, r, :, :, quad * LANES : (quad + 1) * LANES]
            tile = jnp.swapaxes(tile.astype(jnp.float32), 0, 1).astype(jnp.bfloat16)
            target[:, quad * peers : (quad + 1) * peers, :] = tile
        for link, (there, _, _) in enumerate(links):
            guarded(there, lambda link=link: hand(link, slot, r).start())

    def arrived(r):
        for side, (there, _, _) in enumerate(origins):
            block = near_last.at[side] if r == last else near.at[side, :, r]
            guarded(there, pltpu.make_async_copy(block, block, near_recv.at[side, r]).wait)

    def handed(r):
        for link, (there, _, _) in enumerate(links):
            guarded(there, pltpu.make_async_copy(own_last, own_last, near_send.at[link, r]).wait)

    def screen(r):
        arrived(r)
        handed(r)
        for first in range(0, local, 2):
            pairs = []
            for e in (first, first + 1):
                rows = []
                for slot in range(slots):
                    rows.append(own[slot, r, e])
                    rows.extend(near[side, slot, r, e] for side in range(sides))
                pairs.append(jnp.concatenate(rows, 0))
            for j, block in enumerate(products(weights, pairs)):
                for slot in range(slots):
                    done[r, first + j, slot] = block[slot * orbitals : (slot + 1) * orbitals]

    def collect_slot(slot, carry):
        for r in range(radix):
            collect(slot, r)
        return carry

    lax.fori_loop(0, slots - 1, collect_slot, 0)
    rest = pl.ds(0, peers - 1)
    for which in range(2):
        pltpu.make_async_copy(
            send.at[which, :, rest], send.at[which, :, rest], send_sem.at[which]
        ).wait()
    for r in range(radix):
        collect(slots - 1, r)
        if r > 0:
            screen(r - 1)
    pltpu.make_async_copy(send.at[0, :, rest], send.at[0, :, rest], back_send.at[0]).wait()
    arrived(last)
    handed(last)


def products(weights, pairs):
    both = jnp.dot(weights[...], jnp.concatenate(pairs, 1), preferred_element_type=jnp.float32)
    both = both.astype(jnp.bfloat16)
    return [both[:, j * LANES : (j + 1) * LANES] for j in range(len(pairs))]


def finish_kernel(done, own_ref, near_ref, weights, out_hbm, tail, copy_sem, tail_sem):
    slots, local, orbitals, _ = own_ref.shape
    sides = near_ref.shape[0] if weights.shape[1] > slots * orbitals else 0
    last = out_hbm.shape[1] - 1
    share = local // 4
    copies = [
        pltpu.make_async_copy(
            done.at[r, pl.ds(half * share, share)],
            out_hbm.at[pl.ds(half * share, share), r],
            copy_sem.at[r, half],
        )
        for r in range(last)
        for half in range(4)
    ]
    for copy in copies:
        copy.start()
    for half in range(4):
        for first in range(half * share, (half + 1) * share, 2):
            pairs = []
            for e in (first, first + 1):
                rows = []
                for slot in range(slots):
                    rows.append(own_ref[slot, e])
                    rows.extend(near_ref[side, slot, e] for side in range(sides))
                pairs.append(jnp.concatenate(rows, 0))
            for j, block in enumerate(products(weights, pairs)):
                for slot in range(slots):
                    tail[first + j, slot] = block[slot * orbitals : (slot + 1) * orbitals]
        some = pl.ds(half * share, share)
        copies.append(
            pltpu.make_async_copy(tail.at[some], out_hbm.at[some, last], tail_sem.at[half])
        )
        copies[-1].start()
    for copy in copies:
        copy.wait()


def shards(g_less, g_greater, coulomb, pattern):
    e_local, _, slots, orbitals, cols = g_less.shape
    peers, rows = lax.axis_size("energy"), lax.axis_size("slab")
    count = e_local * peers
    radix = 4 if e_local % 64 == 0 else 1
    part = count // radix
    local = e_local // radix
    wide = orbitals // peers * cols
    sides = min(rows - 1, 2)
    forward, inverse = split_tables(count, radix)
    shape = (local, radix, slots, orbitals, cols)
    hbm = pl.BlockSpec(memory_space=pltpu.HBM)
    bf16 = jnp.bfloat16
    dma = pltpu.SemaphoreType.DMA
    operands = (g_less.reshape(shape), g_greater.reshape(shape), coulomb[0], pattern, forward, inverse)
    pin = lambda array: pltpu.with_memory_space_constraint(array, pltpu.HBM)
    kept = max(radix - 1, 1)
    vmem = pl.BlockSpec(memory_space=pltpu.VMEM)
    done, own, near, weights = pl.pallas_call(
        functools.partial(exchange_kernel, peers, rows, radix),
        out_shape=[
            jax.ShapeDtypeStruct((kept, local, slots, orbitals, cols), bf16),
            jax.ShapeDtypeStruct((slots, local, orbitals, cols), bf16),
            jax.ShapeDtypeStruct((max(sides, 1), slots, local, orbitals, cols), bf16),
            jax.ShapeDtypeStruct((slots * orbitals, slots * orbitals * (1 + sides)), bf16),
        ],
        in_specs=[hbm] * 6,
        out_specs=[vmem] * 4,
        scratch_shapes=[
            pltpu.VMEM((2, local, radix, orbitals, cols), bf16),
            pltpu.VMEM((2, slots, peers, radix, local, wide), bf16),
            pltpu.VMEM((2, slots, radix, part, wide), bf16),
            pltpu.VMEM((slots, radix, part, wide), bf16),
            pltpu.VMEM((slots, radix, peers, local, wide), bf16),
            pltpu.VMEM((slots, kept, local, orbitals, cols), bf16),
            pltpu.VMEM((max(sides, 1), slots, kept, local, orbitals, cols), bf16),
            pltpu.VMEM(forward.shape, bf16),
            pltpu.VMEM(inverse.shape, bf16),
            pltpu.VMEM(coulomb.shape[1:], bf16),
            pltpu.SMEM(pattern.shape, jnp.int32),
            dma((2,)), dma((4,)), dma((2,)), dma((2, slots)), dma((1,)), dma((slots, radix)),
            dma((max(sides, 1), radix)), dma((max(sides, 1), radix)),
        ],
        compiler_params=pltpu.CompilerParams(
            collective_id=0, has_side_effects=True, vmem_limit_bytes=44 * 1024 * 1024
        ),
        name="exchange",
    )(*map(pin, operands))
    out = pl.pallas_call(
        finish_kernel,
        out_shape=jax.ShapeDtypeStruct(shape, bf16),
        in_specs=[pl.BlockSpec(memory_space=pl.ANY), vmem, vmem, vmem],
        out_specs=pl.BlockSpec(memory_space=pltpu.HBM),
        scratch_shapes=[
            pltpu.VMEM((local, slots, orbitals, cols), bf16), dma((kept, 4)), dma((4,)),
        ],
        compiler_params=pltpu.CompilerParams(vmem_limit_bytes=16 * 1024 * 1024),
        name="finish",
    )(done, own, near, weights)
    return out.reshape(g_less.shape)


def solution(mesh):
    placed = (
        P("energy", "slab", None, None, None),
        P("energy", "slab", None, None, None),
        P("slab", None, None),
        P(),
    )
    return jax.shard_map(
        shards,
        mesh=mesh,
        in_specs=placed,
        out_specs=P("energy", "slab", None, None, None),
        check_vma=False,
    )
```

```python
import functools
import math

import jax
import jax.numpy as jnp
import numpy as np
from jax import lax
from jax.experimental import pallas as pl
from jax.experimental.pallas import tpu as pltpu
from jax.sharding import PartitionSpec as P

MESH = pl.DeviceIdType.MESH
LANES = 128
TILE = 16


def make_tables(count):
    index = np.arange(count)
    angles = (index[:, None] * index[None, :] % count) * (2.0 * math.pi / count)
    scale = 1.0 / math.sqrt(count)
    table_real = (np.cos(angles) * scale).astype(np.float32).astype(jnp.bfloat16)
    table_imag = (-np.sin(angles) * scale).astype(np.float32).astype(jnp.bfloat16)
    return table_real, table_imag


def split_tables(count, radix):
    part = count // radix
    cut = np.stack(make_tables(count))[:, :part, :].reshape(2, part, part, radix)
    return np.ascontiguousarray(cut.transpose(0, 3, 1, 2)), np.ascontiguousarray(cut.transpose(0, 3, 2, 1))


def turn(values, sign):
    return sign * pltpu.roll(values, LANES // 2, 1)


def guarded(there, action):
    if there is None:
        action()
    else:
        pl.when(there)(action)


def exchange_kernel(
    peers, count, radix, less_hbm, great_hbm, coulomb_hbm, pattern_hbm, fwd_hbm, inv_hbm,
    done, own_last, near_last, weights,
    stage, send, held, reply, back, own, near, fwd_ref, inv_ref, coulomb_ref, pattern_ref,
    load_sem, side_sem, send_sem, recv_sem, back_send, back_recv, near_send, near_recv,
):
    me = lax.axis_index("energy")
    row = lax.axis_index("slab")
    slots = send.shape[1]
    local = send.shape[4]
    wide = send.shape[5]
    quads = wide // LANES
    orbitals = stage.shape[3]
    sides = min(count - 1, 2)
    has_below, has_above = row > 0, row < count - 1

    if count == 2:
        origins = ((None, 1 - row, 2 - 2 * row),)
        links = ((None, 1 - row, 0),)
    elif count > 2:
        origins = (
            (has_below, lax.rem(row + count - 1, count), 0),
            (has_above, lax.rem(row + 1, count), 2),
        )
        links = ((has_above, row + 1, 0), (has_below, row - 1, 1))
    else:
        origins, links = (), ()

    barrier = pltpu.get_barrier_semaphore()
    half = peers // 2

    def partner(step):
        if peers & (peers - 1):
            return lax.rem(me + step + 1, peers)
        odd = lax.rem(step, 2)
        mask = (1 - odd) * half + lax.div(step + odd, 2)
        peer, bit = 0, 1
        while bit < peers:
            peer = peer + bit * lax.rem(lax.div(me, bit) + lax.div(mask, bit), 2)
            bit *= 2
        return peer

    def greet(step, carry):
        pl.semaphore_signal(
            barrier, inc=1, device_id={"energy": partner(step)}, device_id_type=MESH
        )
        return carry

    def load(which, slot, buf):
        source = (less_hbm, great_hbm)[which]
        return pltpu.make_async_copy(source.at[:, :, slot], stage.at[buf], load_sem.at[buf])

    lax.fori_loop(0, peers - 1, greet, 0)
    greeted = peers - 1
    for there, peer, _ in links:
        def meet(peer=peer):
            pl.semaphore_signal(barrier, inc=1, device_id={"slab": peer}, device_id_type=MESH)

        guarded(there, meet)
        greeted = greeted + (1 if there is None else there.astype(jnp.int32))

    load(0, 0, 0).start()
    fetches = [
        pltpu.make_async_copy(source, target, side_sem.at[k])
        for k, (source, target) in enumerate(
            (
                (fwd_hbm, fwd_ref), (inv_hbm, inv_ref),
                (coulomb_hbm, coulomb_ref), (pattern_hbm, pattern_ref),
            )
        )
    ]

    lane = lax.broadcasted_iota(jnp.int32, (1, LANES), 1)
    sign = jnp.where(lane < LANES // 2, -1.0, 1.0).astype(jnp.float32)
    mine = pl.ds(pl.multiple_of(me * local, local), local)

    def scatter(which, slot):
        load(which, slot, which).wait()
        if which == 0:
            load(1, slot, 1).start()
        else:
            @pl.when(slot + 1 < slots)
            def _():
                load(0, slot + 1, 0).start()

        def cut(group, carry):
            top = pl.multiple_of(group * TILE, TILE)
            for r in range(radix):
                tile = stage[which, :, r, pl.ds(top, TILE), :].astype(jnp.float32)
                tile = jnp.swapaxes(tile, 0, 1).astype(jnp.bfloat16)
                for k in range(TILE):
                    send[which, slot, group * (TILE // quads) + k // quads, r, :,
                         (k % quads) * LANES : (k % quads + 1) * LANES] = tile[k]
            return carry

        lax.fori_loop(0, orbitals // TILE, cut, 0)
        if which == 0:
            @pl.when(slot == 0)
            def _():
                for fetch in fetches:
                    fetch.start()
                pl.semaphore_wait(barrier, greeted)

        def ship(step, carry):
            peer = partner(step)
            pltpu.make_async_remote_copy(
                src_ref=send.at[which, slot, peer],
                dst_ref=held.at[which, slot, :, mine, :],
                send_sem=send_sem.at[which],
                recv_sem=recv_sem.at[which, slot],
                device_id={"energy": peer},
                device_id_type=MESH,
            ).start()
            return carry

        lax.fori_loop(0, peers - 1, ship, 0)
        pltpu.make_async_copy(
            send.at[which, slot, me], held.at[which, slot, :, mine, :], recv_sem.at[which, slot]
        ).start()

    def scatter_slot(slot, carry):
        scatter(0, slot)
        scatter(1, slot)
        return carry

    lax.fori_loop(0, slots, scatter_slot, 0)
    for fetch in fetches:
        fetch.wait()

    span = orbitals * (1 + sides)
    depth = slots * span
    entry = lax.broadcasted_iota(jnp.int32, (3 * orbitals, depth), 0)
    place = lax.broadcasted_iota(jnp.int32, (1, depth), 1)
    block = place // orbitals
    inner = lax.rem(place, orbitals)
    column = jnp.full((1, depth), -1, jnp.int32)
    piece = jnp.full((1, depth), 1, jnp.int32)
    for t in range(slots):
        at = t * (1 + sides)
        column = jnp.where(block == at, pattern_ref[row, t], column)
        for side, (there, k, d) in enumerate(origins):
            there = 1 if there is None else there.astype(jnp.int32)
            seen = there * (pattern_ref[k, t] + 1) - 1
            column = jnp.where(block == at + 1 + side, seen, column)
            piece = jnp.where(block == at + 1 + side, d, piece)
    wanted = lax.rem(inner, peers) * quads + inner // peers + piece * orbitals
    for s in range(slots):
        goal = jnp.where(column == pattern_ref[row, s], wanted, -1)
        select = (entry == goal).astype(jnp.float32).astype(jnp.bfloat16)
        part_of = jnp.dot(coulomb_ref[...], select, preferred_element_type=jnp.float32)
        weights[s * orbitals : (s + 1) * orbitals, :] = part_of.astype(jnp.bfloat16)

    for side, (there, _, _) in enumerate(origins):
        if there is not None:
            @pl.when(jnp.logical_not(there))
            def _(side=side):
                near[side] = jnp.zeros(near.shape[1:], near.dtype)
                near_last[side] = jnp.zeros(near_last.shape[1:], near_last.dtype)

    def forward(which, slot, col):
        pieces = []
        for r in range(radix):
            block = held[which, slot, r, :, col]
            direct = jnp.dot(fwd_ref[0, r], block, preferred_element_type=jnp.float32)
            crossed = jnp.dot(fwd_ref[1, r], block, preferred_element_type=jnp.float32)
            pieces.append(direct + turn(crossed, sign))
        if radix == 1:
            return pieces
        even, odd = pieces[0] + pieces[2], pieces[1] + pieces[3]
        gap, twist = pieces[0] - pieces[2], turn(pieces[1] - pieces[3], sign)
        return [even + odd, gap - twist, even - odd, gap + twist]

    def compute(slot, carry):
        for which in range(2):
            pltpu.make_async_copy(
                held.at[which, slot], held.at[which, slot], recv_sem.at[which, slot]
            ).wait()
        for quad in range(quads):
            col = slice(quad * LANES, (quad + 1) * LANES)
            lesser = forward(0, slot, col)
            greater = forward(1, slot, col)
            products = []
            for a, b in zip(lesser, greater):
                along = a * b
                across = a * pltpu.roll(b, LANES // 2, 1)
                products.append(
                    jnp.where(
                        lane < LANES // 2,
                        along + pltpu.roll(along, LANES // 2, 1),
                        across - pltpu.roll(across, LANES // 2, 1),
                    )
                )
            if radix == 4:
                z0, z1, z2, z3 = products
                even, odd = z0 + z2, z1 + z3
                gap, twist = z0 - z2, turn(z1 - z3, sign)
                products = [even + odd, gap + twist, even - odd, gap - twist]
            for r in range(radix):
                block = products[r].astype(jnp.bfloat16)
                direct = jnp.dot(inv_ref[0, r], block, preferred_element_type=jnp.float32)
                crossed = jnp.dot(inv_ref[1, r], block, preferred_element_type=jnp.float32)
                reply[slot, r, :, col] = (direct - turn(crossed, sign)).astype(jnp.bfloat16)

        ending = slot == slots - 1

        def answer(peer, r):
            rows = pl.ds(pl.multiple_of(peer * local, local), local)
            pltpu.make_async_remote_copy(
                src_ref=reply.at[slot, r, rows, :],
                dst_ref=back.at[slot, r, me],
                send_sem=back_send.at[0],
                recv_sem=back_recv.at[slot, r],
                device_id={"energy": peer},
                device_id_type=MESH,
            ).start()

        @pl.when(jnp.logical_and(ending, me > 0))
        def _():
            for r in range(radix):
                answer(0, r)

        for r in range(radix):
            def ship(step, carry, r=r):
                peer = partner(step)

                @pl.when(jnp.logical_or(jnp.logical_not(ending), peer > 0))
                def _():
                    answer(peer, r)
                return carry

            lax.fori_loop(0, peers - 1, ship, 0)
            pltpu.make_async_copy(
                reply.at[slot, r, mine, :], back.at[slot, r, me], back_recv.at[slot, r]
            ).start()
        return carry

    lax.fori_loop(0, slots, compute, 0)

    last = radix - 1

    def hand(link, slot, r):
        _, peer, side = links[link]
        return pltpu.make_async_remote_copy(
            src_ref=own_last.at[slot] if r == last else own.at[slot, r],
            dst_ref=near_last.at[side, slot] if r == last else near.at[side, slot, r],
            send_sem=near_send.at[link, r],
            recv_sem=near_recv.at[side, r],
            device_id={"slab": peer},
            device_id_type=MESH,
        )

    def collect(slot, r):
        pltpu.make_async_copy(back.at[slot, r], back.at[slot, r], back_recv.at[slot, r]).wait()
        target = own_last.at[slot] if r == last else own.at[slot, r]
        for quad in range(quads):
            tile = back[slot, r, :, :, quad * LANES : (quad + 1) * LANES]
            tile = jnp.swapaxes(tile.astype(jnp.float32), 0, 1).astype(jnp.bfloat16)
            target[:, quad * peers : (quad + 1) * peers, :] = tile
        for link, (there, _, _) in enumerate(links):
            guarded(there, lambda link=link: hand(link, slot, r).start())

    def arrived(r):
        for side, (there, _, _) in enumerate(origins):
            block = near_last.at[side] if r == last else near.at[side, :, r]
            guarded(there, pltpu.make_async_copy(block, block, near_recv.at[side, r]).wait)

    def handed(r):
        for link, (there, _, _) in enumerate(links):
            guarded(there, pltpu.make_async_copy(own_last, own_last, near_send.at[link, r]).wait)

    def screen(r):
        arrived(r)
        handed(r)
        for first in range(0, local, 2):
            pairs = []
            for e in (first, first + 1):
                rows = []
                for slot in range(slots):
                    rows.append(own[slot, r, e])
                    rows.extend(near[side, slot, r, e] for side in range(sides))
                pairs.append(jnp.concatenate(rows, 0))
            for j, block in enumerate(products(weights, pairs)):
                for slot in range(slots):
                    done[r, first + j, slot] = block[slot * orbitals : (slot + 1) * orbitals]

    def collect_slot(slot, carry):
        for r in range(radix):
            collect(slot, r)
        return carry

    lax.fori_loop(0, slots - 1, collect_slot, 0)
    rest = pl.ds(0, peers - 1)
    for which in range(2):
        pltpu.make_async_copy(
            send.at[which, :, rest], send.at[which, :, rest], send_sem.at[which]
        ).wait()
    for r in range(radix):
        collect(slots - 1, r)
        if r > 0:
            screen(r - 1)
    pltpu.make_async_copy(send.at[0, :, rest], send.at[0, :, rest], back_send.at[0]).wait()
    arrived(last)
    handed(last)


def products(weights, pairs):
    both = jnp.dot(weights[...], jnp.concatenate(pairs, 1), preferred_element_type=jnp.float32)
    both = both.astype(jnp.bfloat16)
    return [both[:, j * LANES : (j + 1) * LANES] for j in range(len(pairs))]


def finish_kernel(done, own_ref, near_ref, weights, out_hbm, tail, copy_sem, tail_sem):
    slots, local, orbitals, _ = own_ref.shape
    sides = near_ref.shape[0] if weights.shape[1] > slots * orbitals else 0
    last = out_hbm.shape[1] - 1
    share = local // 4
    copies = [
        pltpu.make_async_copy(done.at[r], out_hbm.at[:, r], copy_sem.at[r]) for r in range(last)
    ]
    for copy in copies:
        copy.start()
    for half in range(4):
        for first in range(half * share, (half + 1) * share, 2):
            pairs = []
            for e in (first, first + 1):
                rows = []
                for slot in range(slots):
                    rows.append(own_ref[slot, e])
                    rows.extend(near_ref[side, slot, e] for side in range(sides))
                pairs.append(jnp.concatenate(rows, 0))
            for j, block in enumerate(products(weights, pairs)):
                for slot in range(slots):
                    tail[first + j, slot] = block[slot * orbitals : (slot + 1) * orbitals]
        some = pl.ds(half * share, share)
        copies.append(
            pltpu.make_async_copy(tail.at[some], out_hbm.at[some, last], tail_sem.at[half])
        )
        copies[-1].start()
    for copy in copies:
        copy.wait()


def shards(g_less, g_greater, coulomb, pattern):
    e_local, _, slots, orbitals, cols = g_less.shape
    peers, rows = lax.axis_size("energy"), lax.axis_size("slab")
    count = e_local * peers
    radix = 4 if e_local % 64 == 0 else 1
    part = count // radix
    local = e_local // radix
    wide = orbitals // peers * cols
    sides = min(rows - 1, 2)
    forward, inverse = split_tables(count, radix)
    shape = (local, radix, slots, orbitals, cols)
    hbm = pl.BlockSpec(memory_space=pltpu.HBM)
    bf16 = jnp.bfloat16
    dma = pltpu.SemaphoreType.DMA
    operands = (g_less.reshape(shape), g_greater.reshape(shape), coulomb[0], pattern, forward, inverse)
    pin = lambda array: pltpu.with_memory_space_constraint(array, pltpu.HBM)
    kept = max(radix - 1, 1)
    vmem = pl.BlockSpec(memory_space=pltpu.VMEM)
    done, own, near, weights = pl.pallas_call(
        functools.partial(exchange_kernel, peers, rows, radix),
        out_shape=[
            jax.ShapeDtypeStruct((kept, local, slots, orbitals, cols), bf16),
            jax.ShapeDtypeStruct((slots, local, orbitals, cols), bf16),
            jax.ShapeDtypeStruct((max(sides, 1), slots, local, orbitals, cols), bf16),
            jax.ShapeDtypeStruct((slots * orbitals, slots * orbitals * (1 + sides)), bf16),
        ],
        in_specs=[hbm] * 6,
        out_specs=[vmem] * 4,
        scratch_shapes=[
            pltpu.VMEM((2, local, radix, orbitals, cols), bf16),
            pltpu.VMEM((2, slots, peers, radix, local, wide), bf16),
            pltpu.VMEM((2, slots, radix, part, wide), bf16),
            pltpu.VMEM((slots, radix, part, wide), bf16),
            pltpu.VMEM((slots, radix, peers, local, wide), bf16),
            pltpu.VMEM((slots, kept, local, orbitals, cols), bf16),
            pltpu.VMEM((max(sides, 1), slots, kept, local, orbitals, cols), bf16),
            pltpu.VMEM(forward.shape, bf16),
            pltpu.VMEM(inverse.shape, bf16),
            pltpu.VMEM(coulomb.shape[1:], bf16),
            pltpu.SMEM(pattern.shape, jnp.int32),
            dma((2,)), dma((4,)), dma((2,)), dma((2, slots)), dma((1,)), dma((slots, radix)),
            dma((max(sides, 1), radix)), dma((max(sides, 1), radix)),
        ],
        compiler_params=pltpu.CompilerParams(
            collective_id=0, has_side_effects=True, vmem_limit_bytes=44 * 1024 * 1024
        ),
        name="exchange",
    )(*map(pin, operands))
    out = pl.pallas_call(
        finish_kernel,
        out_shape=jax.ShapeDtypeStruct(shape, bf16),
        in_specs=[pl.BlockSpec(memory_space=pl.ANY), vmem, vmem, vmem],
        out_specs=pl.BlockSpec(memory_space=pltpu.HBM),
        scratch_shapes=[
            pltpu.VMEM((local, slots, orbitals, cols), bf16), dma((kept,)), dma((4,)),
        ],
        compiler_params=pltpu.CompilerParams(vmem_limit_bytes=16 * 1024 * 1024),
        name="finish",
    )(done, own, near, weights)
    return out.reshape(g_less.shape)


def solution(mesh):
    placed = (
        P("energy", "slab", None, None, None),
        P("energy", "slab", None, None, None),
        P("slab", None, None),
        P(),
    )
    return jax.shard_map(
        shards,
        mesh=mesh,
        in_specs=placed,
        out_specs=P("energy", "slab", None, None, None),
        check_vma=False,
    )
```
